32 devices in a mesh: grp: 4 (over y, core), blk: 8 (over z, x).
Axes of the slice: x: 2, y: 2, z: 4, core: 2. Of those that a mesh axis runs over, the one named last changes fastest.
Arguments:
- snapshots: float32 [262144, 256], P(('grp', 'blk')), may hold values from -32 to 32, as said below
- start_basis: float32 [256, 32], replicated, may hold values from -6 to 6
Outputs:
- modes: float32 [262144, 32], P(('grp', 'blk'))
- coefficients: float32 [256, 32], replicated
The draws below stay inside these ranges and needn't reach their ends.
Inputs may be any that keep to these rules, and one draw needn't show every extreme that they name: `snapshots`: real snapshot values of a flow field.
All inputs are finite; a program needn't handle non-finite values.
Results may differ from the reference program's by a relative error of at most 0.0003.
Values sent between devices are 32-bit elements; how exact they have to be, the bound alone decides.
A program may use at most 64 MiB of HBM per device.

```python
import math
import jax
import jax.numpy as jnp
from jax import lax

S = 256
K = 32
P_DEV = 8192
NPTS = 262144
N_GRP = 4
N_BLK = 8


def draw_snapshots(key, part):
    keys = jax.random.split(key, 6)
    times = jnp.arange(S, dtype=jnp.float32)[None, :]
    freq_one = jax.random.uniform(keys[0], (NPTS, 1), jnp.float32, 0.0, 1.0)
    freq_two = jax.random.uniform(keys[1], (NPTS, 1), jnp.float32, 0.0, 1.0)
    phase_one = jax.random.uniform(keys[2], (NPTS, 1), jnp.float32, -math.pi, math.pi)
    phase_two = jax.random.uniform(keys[3], (NPTS, 1), jnp.float32, -math.pi, math.pi)
    amplitude = jnp.exp(jax.random.uniform(keys[4], (NPTS, 1), jnp.float32, math.log(0.5), math.log(1.5)))
    wave = 0.7 * amplitude * (jnp.cos(freq_one * times + phase_one) + jnp.cos(freq_two * times + phase_two))
    noise = jnp.clip(jax.random.normal(keys[5], (NPTS, S), jnp.float32), -4.0, 4.0)
    return wave + noise


def scatter_about(rng, shape, width, limit, kind=jnp.bfloat16):
    values = jax.random.normal(rng, shape, jnp.float32) * width
    return jnp.minimum(jnp.maximum(values, -limit), limit).astype(kind)


def setup_inputs(seed: int = 0) -> dict:
    splits = jax.random.split(jax.random.key(seed), 3)
    snapshots = draw_snapshots(jax.random.fold_in(splits[2], 71), 0)
    start_basis = scatter_about(splits[1], (S, K), 1.0, 6.0, jnp.float32)
    return {"snapshots": snapshots, "start_basis": start_basis}


HIGH = lax.Precision.HIGHEST

def orthonormal(cols):
    count = cols.shape[1]
    finished_list = []
    for j in range(count):
        vector = cols[:, j]
        if finished_list:
            finished = jnp.stack(finished_list, 0)
            for _ in range(2):
                proj = jnp.dot(finished, vector, precision=HIGH)
                vector = vector - jnp.dot(proj, finished, precision=HIGH)
        vector = vector / jnp.sqrt(jnp.sum(vector * vector) + 1e-06)
        finished_list.append(vector)
    return jnp.stack(finished_list, 1)

def block_factor(block, start_basis):
    gram = lax.dot_general(block, block, (((0,), (0,)), ((), ())), precision=HIGH)
    local_basis = orthonormal(jnp.dot(gram, start_basis, precision=HIGH))
    return jnp.dot(gram, local_basis, precision=HIGH) / P_DEV

def reference(snapshots, start_basis):
    blocks = snapshots.reshape(N_GRP, N_BLK, P_DEV, S)

    def group_factor(group_blocks):
        factors = lax.map(lambda b: block_factor(b, start_basis), group_blocks)
        group_gram = jnp.einsum('bsk,btk->st', factors, factors, precision=HIGH) / N_BLK
        group_basis = orthonormal(jnp.dot(group_gram, start_basis, precision=HIGH))
        return jnp.dot(group_gram, group_basis, precision=HIGH)
    group_factors = lax.map(group_factor, blocks)
    total_gram = jnp.einsum('gsk,gtk->st', group_factors, group_factors, precision=HIGH) / N_GRP
    coefficients = orthonormal(jnp.dot(total_gram, start_basis, precision=HIGH))
    modes = jnp.dot(snapshots, coefficients, precision=HIGH)
    return (modes, coefficients)
```

```python
import functools

import jax
import jax.numpy as jnp
from jax import lax
from jax.experimental import pallas as pl
from jax.experimental.pallas import tpu as pltpu
from jax.sharding import PartitionSpec as P

HIGH = lax.Precision.HIGHEST
F32 = jnp.float32
BF16 = jnp.bfloat16
MESH = pl.DeviceIdType.MESH
EPS = 1e-06
CHUNKS = 8


def product(a, b, contract, precision=HIGH):
    return lax.dot_general(
        a, b, (contract, ((), ())), precision=precision, preferred_element_type=F32
    )


def lane_sum(x):
    return jnp.sum(x, axis=1, keepdims=True)


def orthonormal_rows(rows_ref):
    rows = rows_ref[...]
    count = rows.shape[0]
    index = lax.broadcasted_iota(jnp.int32, (count, 1), 0)

    def step(j, state):
        done, left, vector, ahead, leak = state
        following = rows_ref[pl.ds(jnp.minimum(j + 1, count - 1), 1), :]
        overlap = lane_sum(done * vector)
        cross = lane_sum(rows * vector)
        size = lane_sum(vector * vector)
        near = lane_sum(vector * ahead)
        along = lane_sum(vector * following)
        scale = 1.0 / jnp.sqrt(size + EPS)
        unit = vector * scale
        first = along * scale
        second = leak - (first * scale) * overlap
        own = near * scale - first * (scale * scale * size)
        new_vector = (
            ahead
            - unit * (first + own)
            - jnp.sum(done * second, axis=0, keepdims=True)
        )
        new_left = left - unit * (cross * scale)
        new_ahead = jnp.sum(
            jnp.where(index == j + 2, new_left, 0.0), axis=0, keepdims=True
        )
        new_done = jnp.where(index == j, unit, done)
        new_leak = lane_sum(new_done * new_ahead)
        return new_done, new_left, new_vector, new_ahead, new_leak

    state = (
        jnp.zeros_like(rows),
        rows,
        rows[0:1],
        rows[1:2],
        jnp.zeros((count, 1), F32),
    )
    return lax.fori_loop(0, count, step, state)[0]


def kernel(
    n_blk,
    n_grp,
    snap_ref,
    start_ref,
    modes_ref,
    coef_ref,
    snap,
    high,
    low,
    gram,
    rows_ref,
    factors,
    groups,
    load_sem,
    blk_send,
    blk_recv,
    grp_send,
    grp_recv,
):
    points = snap_ref.shape[0]
    count = start_ref.shape[0]
    chunk = points // CHUNKS
    size = snap_ref.shape[1]

    loads = [
        pltpu.make_async_copy(
            snap_ref.at[pl.ds(i * chunk, chunk), :],
            snap.at[pl.ds(i * chunk, chunk), :],
            load_sem.at[i],
        )
        for i in range(CHUNKS)
    ]
    for load in loads:
        load.start()

    me_blk = lax.axis_index("blk")
    me_grp = lax.axis_index("grp")
    barrier = pltpu.get_barrier_semaphore()
    for o in range(1, n_blk):
        peer = lax.rem(me_blk + o, n_blk)
        pl.semaphore_signal(
            barrier, inc=1, device_id={"blk": peer}, device_id_type=MESH
        )
    for o in range(1, n_grp):
        peer = lax.rem(me_grp + o, n_grp)
        pl.semaphore_signal(
            barrier, inc=1, device_id={"grp": peer}, device_id_type=MESH
        )

    def exchange(axis, n, me, buffer, send_sem, recv_sem):
        copies = []
        for o in range(1, n):
            copy = pltpu.make_async_remote_copy(
                src_ref=buffer.at[me],
                dst_ref=buffer.at[me],
                send_sem=send_sem.at[o],
                recv_sem=recv_sem.at[o],
                device_id={axis: lax.rem(me + o, n)},
                device_id_type=MESH,
            )
            copy.start()
            copies.append(copy)
        for o in range(1, n):
            source = lax.rem(me + n - o, n)
            pltpu.make_async_remote_copy(
                src_ref=buffer.at[source],
                dst_ref=buffer.at[source],
                send_sem=send_sem.at[o],
                recv_sem=recv_sem.at[o],
                device_id={axis: lax.rem(me + o, n)},
                device_id_type=MESH,
            ).wait_recv()
        return copies

    gram[...] = jnp.zeros_like(gram)
    for i in range(CHUNKS):
        loads[i].wait()
        part = pl.ds(i * chunk, chunk)
        x = snap[part, :]
        x_high = x.astype(BF16)
        x_low = (x - x_high.astype(F32)).astype(BF16)
        high[part, :] = x_high
        low[part, :] = x_low
        pair = jnp.concatenate([x_high, x_low], axis=1)
        gram[...] += product(x_high, pair, ((0,), (0,)), None)
    mixed = gram[:, size:]
    full = gram[:, :size] + (mixed + mixed.T)

    start = start_ref[...]
    rows_ref[...] = product(start, full, ((1,), (0,)))
    basis = orthonormal_rows(rows_ref)
    factors[me_blk] = product(basis, full, ((1,), (0,))) * (1.0 / points)
    pl.semaphore_wait(barrier, n_blk - 1 + n_grp - 1)
    sent = exchange("blk", n_blk, me_blk, factors, blk_send, blk_recv)

    stacked = factors[...].reshape(n_blk * count, size)
    group_gram = product(stacked, stacked, ((0,), (0,))) * (1.0 / n_blk)
    rows_ref[...] = product(start, group_gram, ((1,), (0,)))
    basis = orthonormal_rows(rows_ref)
    groups[me_grp] = product(basis, group_gram, ((1,), (0,)))
    sent += exchange("grp", n_grp, me_grp, groups, grp_send, grp_recv)

    stacked = groups[...].reshape(n_grp * count, size)
    inner = product(start, stacked, ((1,), (1,)))
    rows_ref[...] = product(inner, stacked, ((1,), (0,))) * (1.0 / n_grp)
    coef = orthonormal_rows(rows_ref)
    coef_ref[...] = coef

    c_high = coef.astype(BF16)
    c_low = (coef - c_high.astype(F32)).astype(BF16)
    pair = jnp.concatenate([c_high, c_low], axis=0)
    for i in range(CHUNKS):
        part = pl.ds(i * chunk, chunk)
        two = product(pair, high[part, :], ((1,), (1,)), None)
        one = product(c_high, low[part, :], ((1,), (1,)), None)
        modes_ref[:, part] = two[:count] + (two[count:] + one)
    for copy in sent:
        copy.wait_send()


def body(n_blk, n_grp, snapshots, start_basis):
    points, size = snapshots.shape
    count = start_basis.shape[1]
    vmem = pl.BlockSpec(memory_space=pltpu.VMEM)
    modes, coef = pl.pallas_call(
        functools.partial(kernel, n_blk, n_grp),
        out_shape=(
            jax.ShapeDtypeStruct((count, points), F32),
            jax.ShapeDtypeStruct((count, size), F32),
        ),
        in_specs=[pl.BlockSpec(memory_space=pltpu.HBM), vmem],
        out_specs=(vmem, vmem),
        scratch_shapes=[
            pltpu.VMEM((points, size), F32),
            pltpu.VMEM((points, size), BF16),
            pltpu.VMEM((points, size), BF16),
            pltpu.VMEM((size, 2 * size), F32),
            pltpu.VMEM((count, size), F32),
            pltpu.VMEM((n_blk, count, size), F32),
            pltpu.VMEM((n_grp, count, size), F32),
            pltpu.SemaphoreType.DMA((CHUNKS,)),
            pltpu.SemaphoreType.DMA((n_blk,)),
            pltpu.SemaphoreType.DMA((n_blk,)),
            pltpu.SemaphoreType.DMA((n_grp,)),
            pltpu.SemaphoreType.DMA((n_grp,)),
        ],
        compiler_params=pltpu.CompilerParams(
            collective_id=0, has_side_effects=True, vmem_limit_bytes=44 * 2**20
        ),
        name="pod",
    )(snapshots, start_basis.T)
    return modes.T, coef.T


def solution(mesh):
    return jax.shard_map(
        functools.partial(body, mesh.shape["blk"], mesh.shape["grp"]),
        mesh=mesh,
        in_specs=(P(("grp", "blk"), None), P()),
        out_specs=(P(("grp", "blk"), None), P()),
        check_vma=False,
    )
```

```python
import functools

import jax
import jax.numpy as jnp
from jax import lax
from jax.experimental import pallas as pl
from jax.experimental.pallas import tpu as pltpu
from jax.sharding import PartitionSpec as P

HIGH = lax.Precision.HIGHEST
F32 = jnp.float32
BF16 = jnp.bfloat16
MESH = pl.DeviceIdType.MESH
EPS = 1e-06
CHUNKS = 8


def product(a, b, contract, precision=HIGH):
    return lax.dot_general(
        a, b, (contract, ((), ())), precision=precision, preferred_element_type=F32
    )


def lane_sum(x):
    return jnp.sum(x, axis=1, keepdims=True)


def sublane_sum(x):
    return jnp.sum(x, axis=0, keepdims=True)


def orthonormal_rows(rows):
    count = rows.shape[0]
    blocks = count // 8
    place = lax.broadcasted_iota(jnp.int32, (8, 1), 0)
    mixed = [rows[8 * b : 8 * b + 8] for b in range(blocks)]
    left = list(mixed)
    vector, ahead = rows[0:1], rows[1:2]
    leak = [None] * blocks
    for j in range(count):
        own_block, own_place = divmod(j, 8)
        size = lane_sum(vector * vector)
        scale = lax.rsqrt(size + EPS)
        unit = vector * scale
        if j == count - 1:
            mixed[own_block] = jnp.where(place == own_place, unit, mixed[own_block])
            break
        dots = [lane_sum(block * vector) for block in mixed]
        near = lane_sum(vector * ahead)
        first = lane_sum(vector * rows[j + 1 : j + 2]) * scale
        own = near * scale - first * (scale * scale * size)
        new_vector = ahead - unit * (first + own)
        again = None
        for b in range((j + 7) // 8):
            second = dots[b] * (-first * scale)
            if leak[b] is not None:
                second = second + leak[b]
            if 8 * b + 8 > j:
                second = jnp.where(place < j - 8 * b, second, 0.0)
            term = mixed[b] * second
            again = term if again is None else again + term
        if again is not None:
            new_vector = new_vector - sublane_sum(again)
        mixed[own_block] = jnp.where(place == own_place, unit, mixed[own_block])
        if j + 2 < count:
            for b in range((j + 2) // 8, blocks):
                left[b] = left[b] - unit * (dots[b] * scale)
            b, p = divmod(j + 2, 8)
            ahead = left[b][p : p + 1]
            leak = [
                lane_sum(mixed[b] * ahead) if b <= own_block else None
                for b in range(blocks)
            ]
        vector = new_vector
    return jnp.concatenate(mixed, axis=0)


def kernel(
    n_blk,
    n_grp,
    snap_ref,
    start_ref,
    modes_ref,
    coef_ref,
    snap,
    high,
    low,
    gram,
    factors,
    groups,
    load_sem,
    blk_send,
    blk_recv,
    grp_send,
    grp_recv,
):
    points = snap_ref.shape[0]
    count = start_ref.shape[0]
    chunk = points // CHUNKS
    size = snap_ref.shape[1]

    loads = [
        pltpu.make_async_copy(
            snap_ref.at[pl.ds(i * chunk, chunk), :],
            snap.at[pl.ds(i * chunk, chunk), :],
            load_sem.at[i],
        )
        for i in range(CHUNKS)
    ]
    for load in loads:
        load.start()

    me_blk = lax.axis_index("blk")
    me_grp = lax.axis_index("grp")
    barrier = pltpu.get_barrier_semaphore()
    for o in range(1, n_blk):
        peer = lax.rem(me_blk + o, n_blk)
        pl.semaphore_signal(
            barrier, inc=1, device_id={"blk": peer}, device_id_type=MESH
        )
    for o in range(1, n_grp):
        peer = lax.rem(me_grp + o, n_grp)
        pl.semaphore_signal(
            barrier, inc=1, device_id={"grp": peer}, device_id_type=MESH
        )

    def exchange(axis, n, me, buffer, send_sem, recv_sem):
        copies = []
        for o in range(1, n):
            copy = pltpu.make_async_remote_copy(
                src_ref=buffer.at[me],
                dst_ref=buffer.at[me],
                send_sem=send_sem.at[o],
                recv_sem=recv_sem.at[o],
                device_id={axis: lax.rem(me + o, n)},
                device_id_type=MESH,
            )
            copy.start()
            copies.append(copy)
        for o in range(1, n):
            source = lax.rem(me + n - o, n)
            pltpu.make_async_remote_copy(
                src_ref=buffer.at[source],
                dst_ref=buffer.at[source],
                send_sem=send_sem.at[o],
                recv_sem=recv_sem.at[o],
                device_id={axis: lax.rem(me + o, n)},
                device_id_type=MESH,
            ).wait_recv()
        return copies

    gram[...] = jnp.zeros_like(gram)
    for i in range(CHUNKS):
        loads[i].wait()
        part = pl.ds(i * chunk, chunk)
        x = snap[part, :]
        x_high = x.astype(BF16)
        x_low = (x - x_high.astype(F32)).astype(BF16)
        high[part, :] = x_high
        low[part, :] = x_low
        pair = jnp.concatenate([x_high, x_low], axis=1)
        gram[...] += product(x_high, pair, ((0,), (0,)), None)
    mixed = gram[:, size:]
    full = gram[:, :size] + (mixed + mixed.T)

    start = start_ref[...]
    basis = orthonormal_rows(product(start, full, ((1,), (0,))))
    factors[me_blk] = product(basis, full, ((1,), (0,))) * (1.0 / points)
    pl.semaphore_wait(barrier, n_blk - 1 + n_grp - 1)
    sent = exchange("blk", n_blk, me_blk, factors, blk_send, blk_recv)

    stacked = factors[...].reshape(n_blk * count, size)
    group_gram = product(stacked, stacked, ((0,), (0,))) * (1.0 / n_blk)
    basis = orthonormal_rows(product(start, group_gram, ((1,), (0,))))
    groups[me_grp] = product(basis, group_gram, ((1,), (0,)))
    sent += exchange("grp", n_grp, me_grp, groups, grp_send, grp_recv)

    stacked = groups[...].reshape(n_grp * count, size)
    inner = product(start, stacked, ((1,), (1,)))
    total = product(inner, stacked, ((1,), (0,))) * (1.0 / n_grp)
    coef = orthonormal_rows(total)
    coef_ref[...] = coef

    c_high = coef.astype(BF16)
    c_low = (coef - c_high.astype(F32)).astype(BF16)
    pair = jnp.concatenate([c_high, c_low], axis=0)
    for i in range(CHUNKS):
        part = pl.ds(i * chunk, chunk)
        two = product(pair, high[part, :], ((1,), (1,)), None)
        one = product(c_high, low[part, :], ((1,), (1,)), None)
        modes_ref[:, part] = two[:count] + (two[count:] + one)
    for copy in sent:
        copy.wait_send()


def body(n_blk, n_grp, snapshots, start_basis):
    points, size = snapshots.shape
    count = start_basis.shape[1]
    vmem = pl.BlockSpec(memory_space=pltpu.VMEM)
    modes, coef = pl.pallas_call(
        functools.partial(kernel, n_blk, n_grp),
        out_shape=(
            jax.ShapeDtypeStruct((count, points), F32),
            jax.ShapeDtypeStruct((count, size), F32),
        ),
        in_specs=[pl.BlockSpec(memory_space=pltpu.HBM), vmem],
        out_specs=(vmem, vmem),
        scratch_shapes=[
            pltpu.VMEM((points, size), F32),
            pltpu.VMEM((points, size), BF16),
            pltpu.VMEM((points, size), BF16),
            pltpu.VMEM((size, 2 * size), F32),
            pltpu.VMEM((n_blk, count, size), F32),
            pltpu.VMEM((n_grp, count, size), F32),
            pltpu.SemaphoreType.DMA((CHUNKS,)),
            pltpu.SemaphoreType.DMA((n_blk,)),
            pltpu.SemaphoreType.DMA((n_blk,)),
            pltpu.SemaphoreType.DMA((n_grp,)),
            pltpu.SemaphoreType.DMA((n_grp,)),
        ],
        compiler_params=pltpu.CompilerParams(
            collective_id=0, has_side_effects=True, vmem_limit_bytes=58 * 2**20
        ),
        name="pod",
    )(snapshots, start_basis.T)
    return modes.T, coef.T


def solution(mesh):
    return jax.shard_map(
        functools.partial(body, mesh.shape["blk"], mesh.shape["grp"]),
        mesh=mesh,
        in_specs=(P(("grp", "blk"), None), P()),
        out_specs=(P(("grp", "blk"), None), P()),
        check_vma=False,
    )
```

```python
import functools

import jax
import jax.numpy as jnp
from jax import lax
from jax.experimental import pallas as pl
from jax.experimental.pallas import tpu as pltpu
from jax.sharding import PartitionSpec as P

HIGH = lax.Precision.HIGHEST
F32 = jnp.float32
BF16 = jnp.bfloat16
MESH = pl.DeviceIdType.MESH
EPS = 1e-06
CHUNKS = 8


def product(a, b, contract, precision=HIGH):
    return lax.dot_general(
        a, b, (contract, ((), ())), precision=precision, preferred_element_type=F32
    )


def lane_sum(x):
    return jnp.sum(x, axis=1, keepdims=True)


def sublane_sum(x):
    return jnp.sum(x, axis=0, keepdims=True)


def orthonormal_rows(rows):
    count = rows.shape[0]
    blocks = count // 8
    place = lax.broadcasted_iota(jnp.int32, (8, 1), 0)
    mixed = [rows[8 * b : 8 * b + 8] for b in range(blocks)]
    left = list(mixed)
    vector, ahead = rows[0:1], rows[1:2]
    leak = [None] * blocks
    for j in range(count):
        own_block, own_place = divmod(j, 8)
        size = lane_sum(vector * vector)
        scale = lax.rsqrt(size + EPS)
        unit = vector * scale
        if j == count - 1:
            mixed[own_block] = jnp.where(place == own_place, unit, mixed[own_block])
            break
        dots = [lane_sum(block * vector) for block in mixed]
        near = lane_sum(vector * ahead)
        first = lane_sum(vector * rows[j + 1 : j + 2]) * scale
        own = near * scale - first * (scale * scale * size)
        new_vector = ahead - unit * (first + own)
        again = None
        for b in range((j + 7) // 8):
            second = dots[b] * (-first * scale)
            if leak[b] is not None:
                second = second + leak[b]
            if 8 * b + 8 > j:
                second = jnp.where(place < j - 8 * b, second, 0.0)
            term = mixed[b] * second
            again = term if again is None else again + term
        if again is not None:
            new_vector = new_vector - sublane_sum(again)
        mixed[own_block] = jnp.where(place == own_place, unit, mixed[own_block])
        if j + 2 < count:
            for b in range((j + 2) // 8, blocks):
                left[b] = left[b] - unit * (dots[b] * scale)
            b, p = divmod(j + 2, 8)
            ahead = left[b][p : p + 1]
            leak = [
                lane_sum(mixed[b] * ahead) if b <= own_block else None
                for b in range(blocks)
            ]
        vector = new_vector
    return jnp.concatenate(mixed, axis=0)


def kernel(
    n_blk,
    n_grp,
    snap_ref,
    start_ref,
    modes_ref,
    coef_ref,
    snap,
    high,
    low,
    gram,
    factors,
    groups,
    load_sem,
    blk_send,
    blk_recv,
    grp_send,
    grp_recv,
):
    points = snap_ref.shape[0]
    count = start_ref.shape[0]
    chunk = points // CHUNKS
    size = snap_ref.shape[1]

    loads = [
        pltpu.make_async_copy(
            snap_ref.at[pl.ds(i * chunk, chunk), :],
            snap.at[pl.ds(i * chunk, chunk), :],
            load_sem.at[i],
        )
        for i in range(CHUNKS)
    ]
    for load in loads:
        load.start()

    me_blk = lax.axis_index("blk")
    me_grp = lax.axis_index("grp")
    barrier = pltpu.get_barrier_semaphore()
    for o in range(1, n_blk):
        peer = lax.rem(me_blk + o, n_blk)
        pl.semaphore_signal(
            barrier, inc=1, device_id={"blk": peer}, device_id_type=MESH
        )
    for o in range(1, n_grp):
        peer = lax.rem(me_grp + o, n_grp)
        pl.semaphore_signal(
            barrier, inc=1, device_id={"grp": peer}, device_id_type=MESH
        )

    def send(buffer, slot, send_sem, recv_sem, target):
        return pltpu.make_async_remote_copy(
            src_ref=buffer.at[slot],
            dst_ref=buffer.at[slot],
            send_sem=send_sem,
            recv_sem=recv_sem,
            device_id=target,
            device_id_type=MESH,
        )

    def exchange(n, me, buffer, send_sem, recv_sem, axis):
        inner = 2 if n % 2 == 0 else 1
        outer = n // inner
        line = me // inner
        spot = me % inner
        across = {axis: line * inner + (inner - 1 - spot)}
        sent = []
        for o in range(1, outer):
            target = {axis: lax.rem(line + o, outer) * inner + spot}
            sent.append(send(buffer, me, send_sem.at[o], recv_sem.at[o], target))
        if inner == 2:
            sent.append(send(buffer, me, send_sem.at[outer], recv_sem.at[outer], across))
        for copy in sent:
            copy.start()
        for o in range(1, outer):
            source = lax.rem(line + outer - o, outer) * inner
            slot = source + spot
            send(buffer, slot, send_sem.at[o], recv_sem.at[o], across).wait_recv()
            if inner == 2:
                place = outer + o
                forward = send(
                    buffer, slot, send_sem.at[place], recv_sem.at[place], across
                )
                forward.start()
                sent.append(forward)
        if inner == 2:
            for o in range(outer):
                source = lax.rem(line + outer - o, outer) * inner
                slot = source + 1 - spot
                place = outer + o
                send(
                    buffer, slot, send_sem.at[place], recv_sem.at[place], across
                ).wait_recv()
        return sent

    def spread(n, me, buffer, send_sem, recv_sem, axis):
        sent = []
        for o in range(1, n):
            target = {axis: lax.rem(me + o, n)}
            sent.append(send(buffer, me, send_sem.at[o], recv_sem.at[o], target))
        for copy in sent:
            copy.start()
        for o in range(1, n):
            slot = lax.rem(me + n - o, n)
            target = {axis: lax.rem(me + o, n)}
            send(buffer, slot, send_sem.at[o], recv_sem.at[o], target).wait_recv()
        return sent

    gram[...] = jnp.zeros_like(gram)
    for i in range(CHUNKS):
        loads[i].wait()
        part = pl.ds(i * chunk, chunk)
        x = snap[part, :]
        x_high = x.astype(BF16)
        x_low = (x - x_high.astype(F32)).astype(BF16)
        high[part, :] = x_high
        low[part, :] = x_low
        pair = jnp.concatenate([x_high, x_low], axis=1)
        gram[...] += product(x_high, pair, ((0,), (0,)), None)
    mixed = gram[:, size:]
    full = gram[:, :size] + (mixed + mixed.T)

    start = start_ref[...]
    basis = orthonormal_rows(product(start, full, ((1,), (0,))))
    factors[me_blk] = product(basis, full, ((1,), (0,))) * (1.0 / points)
    pl.semaphore_wait(barrier, n_blk - 1 + n_grp - 1)
    sent = exchange(n_blk, me_blk, factors, blk_send, blk_recv, "blk")

    stacked = factors[...].reshape(n_blk * count, size)
    inner = product(start, stacked, ((1,), (1,)))
    columns = product(inner, stacked, ((1,), (0,))) * (1.0 / n_blk)
    group_gram = product(stacked, stacked, ((0,), (0,))) * (1.0 / n_blk)
    basis = orthonormal_rows(columns)
    group_factor = product(basis, group_gram, ((1,), (0,)))
    inner = product(columns, basis, ((1,), (1,)))
    groups[me_grp] = product(inner, group_factor, ((1,), (0,)))
    sent += spread(n_grp, me_grp, groups, grp_send, grp_recv, "grp")

    total = groups[0]
    for g in range(1, n_grp):
        total = total + groups[g]
    coef = orthonormal_rows(total * (1.0 / n_grp))
    coef_ref[...] = coef

    c_high = coef.astype(BF16)
    c_low = (coef - c_high.astype(F32)).astype(BF16)
    pair = jnp.concatenate([c_high, c_low], axis=0)
    for i in range(CHUNKS):
        part = pl.ds(i * chunk, chunk)
        two = product(pair, high[part, :], ((1,), (1,)), None)
        one = product(c_high, low[part, :], ((1,), (1,)), None)
        modes_ref[:, part] = two[:count] + (two[count:] + one)
    for copy in sent:
        copy.wait_send()


def body(n_blk, n_grp, snapshots, start_basis):
    points, size = snapshots.shape
    count = start_basis.shape[1]
    vmem = pl.BlockSpec(memory_space=pltpu.VMEM)
    modes, coef = pl.pallas_call(
        functools.partial(kernel, n_blk, n_grp),
        out_shape=(
            jax.ShapeDtypeStruct((count, points), F32),
            jax.ShapeDtypeStruct((count, size), F32),
        ),
        in_specs=[pl.BlockSpec(memory_space=pltpu.HBM), vmem],
        out_specs=(vmem, vmem),
        scratch_shapes=[
            pltpu.VMEM((points, size), F32),
            pltpu.VMEM((points, size), BF16),
            pltpu.VMEM((points, size), BF16),
            pltpu.VMEM((size, 2 * size), F32),
            pltpu.VMEM((n_blk, count, size), F32),
            pltpu.VMEM((n_grp, count, size), F32),
            pltpu.SemaphoreType.DMA((CHUNKS,)),
            pltpu.SemaphoreType.DMA((n_blk,)),
            pltpu.SemaphoreType.DMA((n_blk,)),
            pltpu.SemaphoreType.DMA((n_grp,)),
            pltpu.SemaphoreType.DMA((n_grp,)),
        ],
        compiler_params=pltpu.CompilerParams(
            collective_id=0, has_side_effects=True, vmem_limit_bytes=52 * 2**20
        ),
        name="pod",
    )(snapshots, start_basis.T)
    return modes.T, coef.T


def solution(mesh):
    return jax.shard_map(
        functools.partial(body, mesh.shape["blk"], mesh.shape["grp"]),
        mesh=mesh,
        in_specs=(P(("grp", "blk"), None), P()),
        out_specs=(P(("grp", "blk"), None), P()),
        check_vma=False,
    )
```

```python
import functools

import jax
import jax.numpy as jnp
from jax import lax
from jax.experimental import pallas as pl
from jax.experimental.pallas import tpu as pltpu
from jax.sharding import PartitionSpec as P

HIGH = lax.Precision.HIGHEST
F32 = jnp.float32
BF16 = jnp.bfloat16
MESH = pl.DeviceIdType.MESH
EPS = 1e-06
CHUNKS = 8
PIECES = ((0, 1), (1, 2), (2, 4))


def product(a, b, contract, precision=HIGH):
    return lax.dot_general(
        a, b, (contract, ((), ())), precision=precision, preferred_element_type=F32
    )


def lane_sum(x):
    return jnp.sum(x, axis=1, keepdims=True)


def sublane_sum(x):
    return jnp.sum(x, axis=0, keepdims=True)


def orthonormal_rows(rows, finished=None):
    count = rows.shape[0]
    blocks = count // 8
    place = lax.broadcasted_iota(jnp.int32, (8, 1), 0)
    mixed = [rows[8 * b : 8 * b + 8] for b in range(blocks)]
    left = list(mixed)
    vector, ahead = rows[0:1], rows[1:2]
    leak = [None] * blocks
    for j in range(count):
        own_block, own_place = divmod(j, 8)
        size = lane_sum(vector * vector)
        scale = lax.rsqrt(size + EPS)
        unit = vector * scale
        if j == count - 1:
            mixed[own_block] = jnp.where(place == own_place, unit, mixed[own_block])
            if finished is not None:
                finished(own_block, mixed)
            break
        dots = [lane_sum(block * vector) for block in mixed]
        near = lane_sum(vector * ahead)
        first = lane_sum(vector * rows[j + 1 : j + 2]) * scale
        own = near * scale - first * (scale * scale * size)
        new_vector = ahead - unit * (first + own)
        again = None
        for b in range((j + 7) // 8):
            second = dots[b] * (-first * scale)
            if leak[b] is not None:
                second = second + leak[b]
            if 8 * b + 8 > j:
                second = jnp.where(place < j - 8 * b, second, 0.0)
            term = mixed[b] * second
            again = term if again is None else again + term
        if again is not None:
            new_vector = new_vector - sublane_sum(again)
        mixed[own_block] = jnp.where(place == own_place, unit, mixed[own_block])
        if own_place == 7 and finished is not None:
            finished(own_block, mixed)
        if j + 2 < count:
            for b in range((j + 2) // 8, blocks):
                left[b] = left[b] - unit * (dots[b] * scale)
            b, p = divmod(j + 2, 8)
            ahead = left[b][p : p + 1]
            leak = [
                lane_sum(mixed[b] * ahead) if b <= own_block else None
                for b in range(blocks)
            ]
        vector = new_vector
    return jnp.concatenate(mixed, axis=0)


def kernel(
    n_blk,
    n_grp,
    snap_ref,
    start_ref,
    modes_ref,
    coef_ref,
    snap,
    high,
    low,
    gram,
    factors,
    groups,
    start_vmem,
    start_sem,
    load_sem,
    blk_send,
    blk_recv,
    grp_send,
    grp_recv,
):
    points = snap_ref.shape[0]
    count = start_ref.shape[0]
    chunk = points // CHUNKS
    size = snap_ref.shape[1]

    start_load = pltpu.make_async_copy(start_ref, start_vmem, start_sem)
    start_load.start()
    loads = [
        pltpu.make_async_copy(
            snap_ref.at[pl.ds(i * chunk, chunk), :],
            snap.at[pl.ds(i * chunk, chunk), :],
            load_sem.at[i],
        )
        for i in range(CHUNKS)
    ]
    for load in loads:
        load.start()

    me_blk = lax.axis_index("blk")
    me_grp = lax.axis_index("grp")
    barrier = pltpu.get_barrier_semaphore()
    for o in range(1, n_blk):
        peer = lax.rem(me_blk + o, n_blk)
        pl.semaphore_signal(
            barrier, inc=1, device_id={"blk": peer}, device_id_type=MESH
        )
    for o in range(1, n_grp):
        peer = lax.rem(me_grp + o, n_grp)
        pl.semaphore_signal(
            barrier, inc=1, device_id={"grp": peer}, device_id_type=MESH
        )

    def send(buffer, slot, send_sem, recv_sem, target):
        return pltpu.make_async_remote_copy(
            src_ref=buffer.at[slot],
            dst_ref=buffer.at[slot],
            send_sem=send_sem,
            recv_sem=recv_sem,
            device_id=target,
            device_id_type=MESH,
        )

    def send_rows(slot, piece, o):
        first, last = PIECES[piece]
        part = factors.at[slot, pl.ds(8 * first, 8 * (last - first)), :]
        return pltpu.make_async_remote_copy(
            src_ref=part,
            dst_ref=part,
            send_sem=blk_send.at[piece, o],
            recv_sem=blk_recv.at[piece, o],
            device_id={"blk": lax.rem(me_blk + o, n_blk)},
            device_id_type=MESH,
        )

    def spread(n, me, buffer, send_sem, recv_sem, axis):
        sent = []
        for o in range(1, n):
            target = {axis: lax.rem(me + o, n)}
            sent.append(send(buffer, me, send_sem.at[o], recv_sem.at[o], target))
        for copy in sent:
            copy.start()
        for o in range(1, n):
            slot = lax.rem(me + n - o, n)
            target = {axis: lax.rem(me + o, n)}
            send(buffer, slot, send_sem.at[o], recv_sem.at[o], target).wait_recv()
        return sent

    gram[...] = jnp.zeros_like(gram)
    for i in range(CHUNKS):
        loads[i].wait()
        part = pl.ds(i * chunk, chunk)
        x = snap[part, :]
        x_high = x.astype(BF16)
        x_low = (x - x_high.astype(F32)).astype(BF16)
        high[part, :] = x_high
        low[part, :] = x_low
        pair = jnp.concatenate([x_high, x_low], axis=1)
        gram[...] += product(x_high, pair, ((0,), (0,)), None)
    mixed = gram[:, size:]
    full = gram[:, :size] + (mixed + mixed.T)

    start_load.wait()
    start = start_vmem[...]
    sent = []

    def factor_rows(block, basis):
        for piece, (first, last) in enumerate(PIECES):
            if last != block + 1:
                continue
            rows = jnp.concatenate(basis[first:last], axis=0)
            factors[me_blk, pl.ds(8 * first, 8 * (last - first)), :] = product(
                rows, full, ((1,), (0,))
            ) * (1.0 / points)
            for o in range(1, n_blk):
                copy = send_rows(me_blk, piece, o)
                copy.start()
                sent.append(copy)

    columns = product(start, full, ((1,), (0,)))
    pl.semaphore_wait(barrier, n_blk - 1 + n_grp - 1)
    orthonormal_rows(columns, factor_rows)
    for piece in range(len(PIECES)):
        for o in range(1, n_blk):
            send_rows(lax.rem(me_blk + n_blk - o, n_blk), piece, o).wait_recv()

    stacked = factors[...].reshape(n_blk * count, size)
    inner = product(start, stacked, ((1,), (1,)))
    columns = product(inner, stacked, ((1,), (0,))) * (1.0 / n_blk)
    group_gram = product(stacked, stacked, ((0,), (0,))) * (1.0 / n_blk)
    basis = orthonormal_rows(columns)
    group_factor = product(basis, group_gram, ((1,), (0,)))
    inner = product(columns, basis, ((1,), (1,)))
    groups[me_grp] = product(inner, group_factor, ((1,), (0,)))
    sent += spread(n_grp, me_grp, groups, grp_send, grp_recv, "grp")

    total = groups[0]
    for g in range(1, n_grp):
        total = total + groups[g]
    coef = orthonormal_rows(total * (1.0 / n_grp))
    coef_ref[...] = coef

    c_high = coef.astype(BF16)
    c_low = (coef - c_high.astype(F32)).astype(BF16)
    pair = jnp.concatenate([c_high, c_low], axis=0)
    for i in range(CHUNKS):
        part = pl.ds(i * chunk, chunk)
        two = product(pair, high[part, :], ((1,), (1,)), None)
        one = product(c_high, low[part, :], ((1,), (1,)), None)
        modes_ref[:, part] = two[:count] + (two[count:] + one)
    for copy in sent:
        copy.wait_send()


def body(n_blk, n_grp, snapshots, start_basis):
    points, size = snapshots.shape
    count = start_basis.shape[1]
    vmem = pl.BlockSpec(memory_space=pltpu.VMEM)
    modes, coef = pl.pallas_call(
        functools.partial(kernel, n_blk, n_grp),
        out_shape=(
            jax.ShapeDtypeStruct((count, points), F32),
            jax.ShapeDtypeStruct((count, size), F32),
        ),
        in_specs=[pl.BlockSpec(memory_space=pltpu.HBM)] * 2,
        out_specs=(vmem, vmem),
        scratch_shapes=[
            pltpu.VMEM((points, size), F32),
            pltpu.VMEM((points, size), BF16),
            pltpu.VMEM((points, size), BF16),
            pltpu.VMEM((size, 2 * size), F32),
            pltpu.VMEM((n_blk, count, size), F32),
            pltpu.VMEM((n_grp, count, size), F32),
            pltpu.VMEM((count, size), F32),
            pltpu.SemaphoreType.DMA,
            pltpu.SemaphoreType.DMA((CHUNKS,)),
            pltpu.SemaphoreType.DMA((len(PIECES), n_blk)),
            pltpu.SemaphoreType.DMA((len(PIECES), n_blk)),
            pltpu.SemaphoreType.DMA((n_grp,)),
            pltpu.SemaphoreType.DMA((n_grp,)),
        ],
        compiler_params=pltpu.CompilerParams(
            collective_id=0, has_side_effects=True, vmem_limit_bytes=52 * 2**20
        ),
        name="pod",
    )(snapshots, start_basis.T)
    return modes.T, coef.T


def solution(mesh):
    return jax.shard_map(
        functools.partial(body, mesh.shape["blk"], mesh.shape["grp"]),
        mesh=mesh,
        in_specs=(P(("grp", "blk"), None), P()),
        out_specs=(P(("grp", "blk"), None), P()),
        check_vma=False,
    )
```
